32 devices in a mesh: groups: 2 (over y), rows: 4 (over z), cols: 2 (over x), chan: 2 (over core).
Axes of the slice: x: 2, y: 2, z: 4, core: 2. Of those that a mesh axis runs over, the one named last changes fastest.
Arguments:
- tokens: bfloat16 [128, 128, 192], P(('groups', 'rows'), 'cols', 'chan'), parts along dimension 0, may hold values from -6 to 6
- tile_mask: int32 [2, 2], P('groups'), parts along dimension 0, may hold values 0 or 1
- ln_gain: float32 [192], replicated, may hold values from 0.1 to 1.9
- w_in_x: bfloat16 [192, 384], P(None, 'chan'), may hold values from -0.4375 to 0.4375
- w_in_z: bfloat16 [192, 384], P(None, 'chan'), may hold values from -0.4375 to 0.4375
- conv_w: float32 [3, 3, 384], P(None, None, 'chan'), may hold values from -2 to 2
- conv_b: float32 [384], P('chan'), may hold values from -0.5 to 0.5
- gate_scale: float32 [4, 384], P(None, 'chan'), may hold values from 0.5 to 2
- gate_bias: float32 [4, 384], P(None, 'chan'), may hold values from -8.5 to -1, as said below
- norm_gain: float32 [384], P('chan'), may hold values from 0.1 to 1.9
- w_out: bfloat16 [384, 192], P('chan'), may hold values from -0.3125 to 0.3125
Outputs:
- mixed: bfloat16 [128, 128, 192], P(('groups', 'rows'), 'cols', 'chan'), parts along dimension 0
The draws below stay inside these ranges and needn't reach their ends.
There are 2 independent parts, one for each index of `groups`. The reference program is written for one: setup_inputs(seed, part) draws one part's arguments, and reference() takes and returns one part's arrays. A program takes and returns all parts, laid end to end along the dimension named above; an argument that names none is the same for every part. Nothing has to cross between parts.
Inputs may be any that keep to these rules, and one draw needn't show every extreme that they name: `gate_bias`: for each direction, some channels take values near minus the log of the scan's length and others near minus the log of 30 to 50.
All inputs are finite; a program needn't handle non-finite values.
Results may differ from the reference program's by a relative error of at most 0.009.
Values may be sent and summed in bfloat16 or wider, within the bound.
A program may use at most 64 MiB of HBM per device.

```python
import math
import jax
import jax.numpy as jnp
from jax import lax

C = 192
E = 384
TILE = 64
H = 64
W = 128
N_CHAN = 2


def draw_gate_bias(key, part):
    key_slow, key_long, key_fast = jax.random.split(jax.random.fold_in(key, 41), 3)
    slow_share = 0.5
    slow = jax.random.uniform(key_slow, (4, E), jnp.float32) < slow_share
    lengths = jnp.array([W, W, H, H], jnp.float32)[:, None]
    slow_bias = -jnp.log(lengths * jax.random.uniform(key_long, (4, E), jnp.float32, 0.5, 2.0))
    fast_bias = -jnp.log(jax.random.uniform(key_fast, (4, E), jnp.float32, 30.0, 50.0))
    return jnp.where(slow, slow_bias, fast_bias).astype(jnp.float32)


def place_ends(values, stream_key, smallest, high):
    dims = values.shape
    index_at = [jax.random.randint(jax.random.fold_in(stream_key, axis), (), 0, dims[axis]) for axis in range(len(dims))]
    values = values.at[tuple(index_at)].set(smallest)
    longest = dims.index(max(dims))
    index_at[longest] = (index_at[longest] + 1) % dims[longest]
    return values.at[tuple(index_at)].set(high)


def levels(own_key, shape, cuts, smallest, high):
    level, own = 1.0, jax.random.fold_in(own_key, 6)
    for dim, blocks in cuts:
        draws = jnp.exp(jax.random.uniform(jax.random.fold_in(own, dim), (blocks,), jnp.float32, smallest / len(cuts), high / len(cuts)))
        level = level * jnp.repeat(draws, shape[dim] // blocks).reshape([-1 if axis == dim else 1 for axis in range(len(shape))])
    return level


def noise(key, extent, deviation, most, cuts=(), kind=jnp.bfloat16):
    result = deviation * jax.random.normal(key, extent, jnp.float32)
    if cuts:
        result = result * levels(key, extent, cuts, -0.22, 0.18)
    return jnp.clip(result, -most, most).astype(kind)


def setup_inputs(seed: int = 0, part: int = 0) -> dict:
    key_of = jax.random.split(jax.random.key(seed), 12)
    part_splits = jax.random.split(jax.random.fold_in(key_of[11], part), 12)
    tokens = noise(part_splits[0], (H, W, C), 1.0, 6.0, ((0, 4), (1, 2), (2, 2)))
    tile_mask = place_ends((jax.random.randint(part_splits[1], (H // TILE, W // TILE), 0, 5) < 3).astype(jnp.int32), jax.random.fold_in(part_splits[1], 1), 0, 1)
    ln_gain = jnp.clip(1.0 + 0.18 * jax.random.normal(key_of[2], (C,), jnp.float32), 0.1, 1.9)
    w_in_x = noise(key_of[3], (C, E), C ** -0.5, 0.4375, ((1, 2),))
    w_in_z = noise(key_of[4], (C, E), C ** -0.5, 0.4375, ((1, 2),))
    conv_w = noise(key_of[5], (3, 3, E), 0.4, 2.0, ((2, 2),), jnp.float32)
    conv_b = jnp.clip(jax.random.uniform(key_of[6], (E,), jnp.float32, -0.5, 0.5) * levels(key_of[6], (E,), ((0, 2),), -0.4, 0.0), -0.5, 0.5)
    gate_scale = jnp.clip(jnp.exp(math.log(2.0) - 1.3862944 * jax.random.uniform(key_of[7], (4, E), jnp.float32) ** levels(key_of[7], (4, E), ((1, 2),), -0.2, 0.2)), 0.5, 2.0)
    gate_bias = draw_gate_bias(jax.random.fold_in(key_of[11], 71), part)
    norm_gain = jnp.clip(1.0 + 0.18 * jax.random.normal(key_of[9], (E,), jnp.float32), 0.1, 1.9)
    w_out = noise(key_of[10], (E, C), E ** -0.5, 0.3125, ((0, 2),))
    return {"tokens": tokens, "tile_mask": tile_mask, "ln_gain": ln_gain, "w_in_x": w_in_x, "w_in_z": w_in_z, "conv_w": conv_w, "conv_b": conv_b, "gate_scale": gate_scale, "gate_bias": gate_bias, "norm_gain": norm_gain, "w_out": w_out}


def combine(earlier, later):
    return (earlier[0] * later[0], later[0] * earlier[1] + later[1])

def run_scan(keep, push, axis, backward):
    return lax.associative_scan(combine, (keep, push), axis=axis, reverse=backward)[1]

def reference(tokens, tile_mask, ln_gain, w_in_x, w_in_z, conv_w, conv_b, gate_scale, gate_bias, norm_gain, w_out):
    xfull = tokens.astype(jnp.float32)
    mean = lax.optimization_barrier(jnp.mean(xfull, -1, keepdims=True))
    var = lax.optimization_barrier(jnp.mean((xfull - mean) ** 2, -1, keepdims=True))
    normed = ((xfull - mean) * lax.rsqrt(var + 1e-05) * ln_gain).astype(jnp.bfloat16).reshape(H * W, C)
    u_pre = jnp.dot(normed, w_in_x, preferred_element_type=jnp.float32).astype(jnp.bfloat16).reshape(H, W, E)
    zgate = jnp.dot(normed, w_in_z, preferred_element_type=jnp.float32).reshape(H, W, E)
    mask = jnp.repeat(jnp.repeat(tile_mask, TILE, 0), TILE, 1).astype(jnp.float32)

    def block(index):
        start = index * 64
        piece = lax.dynamic_slice_in_dim(u_pre, start, 64, 2).astype(jnp.float32)
        padded = jnp.pad(piece, ((1, 1), (1, 1), (0, 0)))
        weights = lax.dynamic_slice_in_dim(conv_w, start, 64, 2)
        filtered = jnp.zeros((H, W, 64), jnp.float32) + lax.dynamic_slice_in_dim(conv_b, start, 64, 0)
        for di in range(3):
            for dj in range(3):
                filtered = filtered + weights[di, dj] * padded[di:di + H, dj:dj + W]
        scanned = lax.optimization_barrier(jax.nn.silu(filtered).astype(jnp.bfloat16)).astype(jnp.float32)
        scales = lax.dynamic_slice_in_dim(gate_scale, start, 64, 1)
        biases = lax.dynamic_slice_in_dim(gate_bias, start, 64, 1)
        states = []
        for direction, (axis, backward) in enumerate([(1, False), (1, True), (0, False), (0, True)]):
            gate = mask[:, :, None] * jax.nn.sigmoid(scales[direction] * scanned + biases[direction])
            states.append(run_scan(1.0 - gate, gate * scanned, axis, backward))
        vertical = lax.optimization_barrier((states[2] + states[3]).astype(jnp.bfloat16)).astype(jnp.float32)
        return states[0] + states[1] + vertical
    blocks = lax.map(block, jnp.arange(E // 64, dtype=jnp.int32))
    summed = jnp.transpose(blocks, (1, 2, 0, 3)).reshape(H, W, E)
    inner_mean = lax.optimization_barrier(jnp.sum(summed, -1, keepdims=True)) / E
    inner_msq = lax.optimization_barrier(jnp.sum(summed * summed, -1, keepdims=True)) / E
    scaled = (summed - inner_mean) * lax.rsqrt(inner_msq - inner_mean * inner_mean + 1e-05) * norm_gain
    gated = (scaled * jax.nn.silu(zgate)).astype(jnp.bfloat16).reshape(H * W, E)
    half = E // N_CHAN
    branch = jnp.zeros((H * W, C), jnp.float32)
    for part_index in range(N_CHAN):
        partial_sum = jnp.dot(gated[:, part_index * half:(part_index + 1) * half], w_out[part_index * half:(part_index + 1) * half], preferred_element_type=jnp.float32)
        branch = branch + lax.optimization_barrier(partial_sum.astype(jnp.bfloat16)).astype(jnp.float32)
    mixed = xfull + mask[:, :, None] * branch.reshape(H, W, C)
    return mixed.astype(jnp.bfloat16)
```

```python
import functools

import jax
import jax.numpy as jnp
from jax import lax
from jax.experimental import pallas as pl
from jax.experimental.pallas import tpu as pltpu
from jax.sharding import PartitionSpec as P

TILE = 64
LANES = 128
F32 = jnp.float32
BF16 = jnp.bfloat16
MESH = pl.DeviceIdType.MESH


def ln_pair(own, other, gain_own, gain_other):
    count = own.shape[-1] + other.shape[-1]
    mean = jnp.sum(own + other, -1, keepdims=True) / count
    own = own - mean
    other = other - mean
    var = jnp.sum(own * own + other * other, -1, keepdims=True) / count
    rstd = lax.rsqrt(var + 1e-05)
    return (own * rstd * gain_own).astype(BF16), (other * rstd * gain_other).astype(BF16)


def silu(x):
    half = 0.5 * x
    return half + half * jnp.tanh(half)


def kernel(
    n_rows, n_cols, pitch,
    *refs,
):
    held, out, staged = refs[:11], refs[11], refs[12:23]
    sem_in, sem_ready = refs[23:25]
    body(n_rows, n_cols, pitch, held, staged, sem_in, sem_ready, *staged, out, *refs[25:])


def body(
    n_rows, n_cols, pitch, held, staged, sem_in, sem_ready,
    tok, tile_mask, ln_gain, w_x, w_z, conv_w, conv_b, gate_scale, gate_bias, norm_gain, w_out,
    out,
    tok_other, cells, edge, halo, wx, wz, wo, par, gpar, normed, halo_u, upad, u,
    pv, kv, ph, kh, zs, gated, vtot, packed, vsend, vrecv, hsend, hrecv, cv, ch, st, st_other, psend, precv, pown, bsend, brecv, bown,
    sem_tok, sem_halo_s, sem_halo_r, sem_v_s, sem_v_r, sem_h_s, sem_h_r, sem_st, sem_p, sem_b,
):
    r, c, k = (lax.axis_index(name) for name in ("rows", "cols", "chan"))
    o = 1 - k
    rows, cols, part = tok.shape
    width = w_x.shape[1]
    tiles = wx.shape[-1] // LANES

    def at(dr, dc, chan):
        return {"rows": r + dr, "cols": c + dc, "chan": chan}

    up, down, left, right = r > 0, r < n_rows - 1, c > 0, c < n_cols - 1
    base = 2 * cols
    corner = base + 2 * rows
    neighbours = (
        (up, -1, 0, tok.at[0], cols, cols),
        (down, 1, 0, tok.at[rows - 1], 0, cols),
        (left, 0, -1, edge.at[pl.ds(0, rows)], base + rows, rows),
        (right, 0, 1, edge.at[pl.ds(rows, rows)], base, rows),
        (up & left, -1, -1, tok.at[0, pl.ds(0, 16)], corner + 48, 16),
        (up & right, -1, 1, tok.at[0, pl.ds(cols - 16, 16)], corner + 32, 16),
        (down & left, 1, -1, tok.at[rows - 1, pl.ds(0, 16)], corner + 16, 16),
        (down & right, 1, 1, tok.at[rows - 1, pl.ds(cols - 16, 16)], corner, 16),
    )
    mirror = (1, 0, 3, 2, 7, 6, 5, 4)

    barrier = pltpu.get_barrier_semaphore()
    expected = jnp.int32(1)
    pl.semaphore_signal(barrier, inc=1, device_id=at(0, 0, o), device_id_type=MESH)
    for present, dr, dc, *_rest in neighbours:
        for chan in (k, o):

            @pl.when(present)
            def _():
                pl.semaphore_signal(barrier, inc=1, device_id=at(dr, dc, chan), device_id_type=MESH)

        expected = expected + 2 * present.astype(jnp.int32)

    loads = [pltpu.make_async_copy(held[n], staged[n], sem_in.at[n]) for n in range(len(held))]
    for load in loads:
        load.start()

    for n, (present, *_rest) in enumerate(neighbours):
        start, size = neighbours[mirror[n]][4], neighbours[n][5]

        @pl.when(jnp.logical_not(present))
        def _():
            halo[:, pl.ds(start, size), :] = jnp.zeros((2, size, part), BF16)

    loads[0].wait()
    cells[...] = jnp.zeros(cells.shape, F32)
    for i in range(rows):
        cells[pl.ds(32 * i, 16), 0:part] = tok[i, 0:16, :].astype(F32)
        cells[pl.ds(32 * i + 16, 16), 0:part] = tok[i, cols - 16 : cols, :].astype(F32)
    edge[pl.ds(0, rows), :] = cells[pl.ds(0, rows, stride=32), :][:, 0:part].astype(BF16)
    edge[pl.ds(rows, rows), :] = cells[pl.ds(31, rows, stride=32), :][:, 0:part].astype(BF16)

    pl.semaphore_wait(barrier, expected)

    axes = [(0, n_rows, r, "rows"), (1, n_cols, c, "cols")]

    def pass_on(far):
        for a, count, mine, name in axes:
            for d in range(2 if far < count else 0):
                step = -1 if d else 1
                subject, target = mine + step * (far - 1), mine - step

                @pl.when((subject >= 0) & (subject < count) & (target >= 0) & (target < count))
                def _():
                    pl.semaphore_signal(
                        sem_ready.at[a, d, far], inc=1, device_id={name: target}, device_id_type=MESH
                    )

    def hear(far):
        for a, count, mine, name in axes:
            for d in range(2 if far < count else 0):
                subject = mine + (-far if d else far)

                @pl.when((subject >= 0) & (subject < count))
                def _():
                    pl.semaphore_wait(sem_ready.at[a, d, far], 1)

    most = max(n_rows, n_cols)

    bands = 2
    band = rows // bands

    def tok_copy(g):
        place = pl.ds(g * band, band)
        return pltpu.make_async_remote_copy(
            tok.at[place], tok_other.at[place], sem_tok.at[0, g], sem_tok.at[1, g],
            device_id=at(0, 0, o), device_id_type=MESH,
        )

    for g in range(bands):
        tok_copy(g).start()

    def halo_copy(n, turn, chan):
        _, dr, dc, source, place, size = neighbours[n]
        return pltpu.make_async_remote_copy(
            source,
            halo.at[k, pl.ds(place, size)],
            sem_halo_s.at[n, turn],
            sem_halo_r.at[mirror[n], k],
            device_id=at(dr, dc, chan),
            device_id_type=MESH,
        )

    for n, (present, *_rest) in enumerate(neighbours):

        @pl.when(present)
        def _():
            for turn, chan in enumerate((k, o)):
                halo_copy(n, turn, chan).start()

    pass_on(2)

    for load in loads[1:]:
        load.wait()

    wx[...] = jnp.zeros(wx.shape, BF16)
    wz[...] = jnp.zeros(wz.shape, BF16)
    for slot, chan in enumerate((k, o)):
        place = pl.ds(pl.multiple_of(chan * part, 16), part)
        wx[slot, :, 0:width] = w_x[place, :]
        wz[slot, :, 0:width] = w_z[place, :]
    wo[...] = jnp.zeros(wo.shape, BF16)
    first, second = w_out[:, 0:part].astype(F32), w_out[:, part : 2 * part].astype(F32)
    wo[0:width, 0:part] = jnp.where(k == 0, first, second).astype(BF16)
    wo[0:width, LANES : LANES + part] = jnp.where(k == 0, second, first).astype(BF16)
    par[...] = jnp.zeros(par.shape, F32)
    for di in range(3):
        par[pl.ds(3 * di, 3), 0:width] = conv_w[di]
    par[9:10, 0:width] = conv_b[...]
    par[10:11, 0:width] = norm_gain[...]
    gpar[...] = jnp.zeros(gpar.shape, F32)
    scale, bias = 0.5 * gate_scale[...], 0.5 * gate_bias[...]
    for t in range(tiles):
        lo, hi = t * LANES, min(width, (t + 1) * LANES)
        gpar[t, 0:4, 0 : hi - lo] = scale[:, lo:hi]
        gpar[t, 4:8, 0 : hi - lo] = bias[:, lo:hi]
    gain = ln_gain[...]
    gain_own = jnp.where(k == 0, gain[:, 0:part], gain[:, part : 2 * part])
    gain_other = jnp.where(k == 0, gain[:, part : 2 * part], gain[:, 0:part])
    half_mask = 0.5 * tile_mask[r * rows // TILE, c * cols // TILE].astype(F32)


    def norm_row(i, carry):
        a, b = ln_pair(tok[i].astype(F32), tok_other[i].astype(F32), gain_own, gain_other)
        normed[0, i] = a
        normed[1, i] = b
        return carry

    for g in range(bands):
        tok_copy(g).wait_recv()
        lax.fori_loop(g * band, (g + 1) * band, norm_row, 0, unroll=True)
    step_rows = 4

    def product(q, weights):
        place = pl.ds(q * step_rows, step_rows)
        return jnp.dot(
            normed[0, place].reshape(step_rows * cols, part), weights[0], preferred_element_type=F32
        ) + jnp.dot(
            normed[1, place].reshape(step_rows * cols, part), weights[1], preferred_element_type=F32
        )

    def product_x(q, carry):
        value = product(q, wx).astype(BF16).astype(F32)
        for t in range(tiles):
            upad[t, pl.ds(q * step_rows + 1, step_rows), 8 : 8 + cols, :] = value[
                :, t * LANES : (t + 1) * LANES
            ].reshape(step_rows, cols, LANES)
        return carry

    lax.fori_loop(0, rows // step_rows, product_x, 0, unroll=True)

    for far in range(2, most):
        hear(far)
        pass_on(far + 1)

    for n, (present, *_rest) in enumerate(neighbours):
        place, size = neighbours[mirror[n]][4], neighbours[n][5]

        @pl.when(present)
        def _():
            for chan in (0, 1):
                landed = halo.at[chan, pl.ds(place, size)]
                pltpu.make_async_remote_copy(
                    landed, landed, sem_halo_s.at[n, 0], sem_halo_r.at[n, chan],
                    device_id=at(0, 0, o), device_id_type=MESH,
                ).wait_recv()

    a, b = ln_pair(halo[k].astype(F32), halo[o].astype(F32), gain_own, gain_other)
    ring = jnp.dot(a, wx[0], preferred_element_type=F32) + jnp.dot(b, wx[1], preferred_element_type=F32)
    halo_u[...] = ring.astype(BF16).astype(F32)
    for t in range(tiles):
        lanes = pl.ds(t * LANES, LANES)
        upad[t, 0, 8 : 8 + cols, :] = halo_u[0:cols, lanes]
        upad[t, rows + 1, 8 : 8 + cols, :] = halo_u[cols : 2 * cols, lanes]
        for i in range(rows):
            upad[t, 1 + i, 7:8, :] = halo_u[base + i : base + i + 1, lanes]
            upad[t, 1 + i, 8 + cols : 9 + cols, :] = halo_u[base + rows + i : base + rows + i + 1, lanes]
        upad[t, 0, 7:8, :] = halo_u[corner + 15 : corner + 16, lanes]
        upad[t, 0, 8 + cols : 9 + cols, :] = halo_u[corner + 16 : corner + 17, lanes]
        upad[t, rows + 1, 7:8, :] = halo_u[corner + 47 : corner + 48, lanes]
        upad[t, rows + 1, 8 + cols : 9 + cols, :] = halo_u[corner + 48 : corner + 49, lanes]

    def conv_row(i, carry):
        place = pl.ds(pl.multiple_of(i * pitch, 8), cols)
        for t in range(tiles):
            lanes = pl.ds(t * LANES, LANES)
            total = jnp.broadcast_to(par[9:10, lanes], (cols, LANES))
            for di in range(3):
                for dj in range(3):
                    tap = 3 * di + dj
                    total = total + par[tap : tap + 1, lanes] * upad[t, i + di, 7 + dj : 7 + dj + cols, :]
            u[t, place, :] = silu(total).astype(BF16).astype(F32)
        return carry

    lax.fori_loop(0, rows, conv_row, 0, unroll=2)

    span = 16
    per = cols // span

    def vertical(q, carry):
        t = q // per
        col = pl.multiple_of((q % per) * span, span)
        params = gpar[t]
        state = [[jnp.zeros((span, LANES), F32), jnp.ones((span, LANES), F32)] for _ in range(2)]
        for i in range(rows):
            for d in range(2):
                at_row = rows - 1 - i if d else i
                value = u[t, pl.ds(at_row * pitch + col, span), :]
                gate = half_mask + half_mask * jnp.tanh(params[2 + d : 3 + d] * value + params[6 + d : 7 + d])
                keep = 1.0 - gate
                state[d][0] = keep * state[d][0] + gate * value
                state[d][1] = keep * state[d][1]
                place = pl.ds(at_row * cols + col, span)
                pv[d, t, place, :] = state[d][0]
                kv[d, t, place, :] = state[d][1]
        for d in range(2):
            for j in range(2):
                vtot[d, j, t, pl.ds(col, span), :] = state[d][j]
        return carry

    lax.fori_loop(0, tiles * per, vertical, 0)

    side = lax.broadcasted_iota(jnp.int32, (cols // 2, LANES), 1) < LANES // 2
    for d in range(2):
        for j in range(2):
            vsend[d, j, 0:cols] = vtot[d, j, 0].astype(BF16)
            vsend[d, j, cols : cols + cols // 2] = jnp.where(
                side, vtot[d, j, 1, 0 : cols // 2], pltpu.roll(vtot[d, j, 1, cols // 2 : cols], LANES // 2, 1)
            ).astype(BF16)

    def totals(count, mine, name, sends, recvs, sems, semr, act, d, far):
        target = mine - far if d else mine + far
        outer = mine == count - 1 if d else mine == 0
        present = (target >= 0) & (target < count)
        for whole in (True, False):
            a, b = (sends.at[d], recvs.at[mine]) if whole else (sends.at[d, 0], recvs.at[mine, 0])

            @pl.when(present & (jnp.logical_not(outer) if whole else outer))
            def _():
                act(
                    pltpu.make_async_remote_copy(
                        a, b, sems.at[d, far], semr.at[mine], device_id={name: target}, device_id_type=MESH
                    )
                )

    def all_totals(act, *which):
        for far in range(which[0] - 1, 0, -1):
            for d in range(2):
                totals(*which, act, d, far)

    def gather(count, mine, recvs, sems, semr, total, name):
        total[...] = jnp.zeros(total.shape, F32)
        other = {name: jnp.where(mine == 0, 1, mine - 1)}
        for d in range(2):

            def one(s, carry, d=d):
                source = count - 1 - s if d else s
                ahead = source > mine if d else source < mine

                def wait(ref):
                    pltpu.make_async_remote_copy(
                        ref, ref, sems.at[d, 0], semr.at[source], device_id=other, device_id_type=MESH
                    ).wait_recv()

                @pl.when(ahead & (s == 0))
                def _():
                    wait(recvs.at[source, 0])
                    total[d] = recvs[source, 0].astype(F32)

                @pl.when(ahead & (s > 0))
                def _():
                    wait(recvs.at[source])
                    total[d] = recvs[source, 0].astype(F32) + recvs[source, 1].astype(F32) * total[d]

                return carry

            lax.fori_loop(0, count - 1, one, 0)

    vertical_set = (n_rows, r, "rows", vsend, vrecv, sem_v_s, sem_v_r)
    horizontal_set = (n_cols, c, "cols", hsend, hrecv, sem_h_s, sem_h_r)
    all_totals(lambda copy: copy.start(), *vertical_set)

    hparams = [gpar[t] for t in range(tiles)]

    def horizontal(j, states):
        new = []
        for t in range(tiles):
            for d in range(2):
                pos = cols - 1 - j if d else j
                push, kept = states[2 * t + d]
                place = pl.ds(pos, rows, stride=pitch)
                value = u[t, place, :]
                params = hparams[t]
                gate = half_mask + half_mask * jnp.tanh(params[d : d + 1] * value + params[4 + d : 5 + d])
                keep = 1.0 - gate
                push = keep * push + gate * value
                kept = keep * kept
                ph[d, t, place, :] = push
                kh[d, t, place, :] = kept
                new.append((push, kept))
        return tuple(new)

    start = tuple((jnp.zeros((rows, LANES), F32), jnp.ones((rows, LANES), F32)) for _ in range(2 * tiles))
    states = lax.fori_loop(0, cols, horizontal, start, unroll=4)
    for t in range(tiles):
        for d in range(2):
            for j in range(2):
                hsend[d, j, t] = states[2 * t + d][j].astype(BF16)
    all_totals(lambda copy: copy.start(), *horizontal_set)

    def product_z(q, carry):
        value = silu(product(q, wz)) * par[10:11, :]
        gated[pl.ds(q * step_rows * cols, step_rows * cols), :] = value.astype(BF16)
        for t in range(tiles):
            zs[t, pl.ds(pl.multiple_of(q * step_rows * cols, 8), step_rows * cols), :] = value[
                :, t * LANES : (t + 1) * LANES
            ]
        return carry

    lax.fori_loop(0, rows // step_rows, product_z, 0, unroll=True)

    def scale_copy(q):
        place = pl.ds(q * step_rows, step_rows)
        return pltpu.make_async_remote_copy(
            bsend.at[place], brecv.at[place], sem_b.at[0, q], sem_b.at[1, q],
            device_id=at(0, 0, o), device_id_type=MESH,
        )

    def project(q):
        return jnp.dot(
            gated[pl.ds(q * step_rows * cols, step_rows * cols), :], wo[...], preferred_element_type=F32
        )

    chunks = rows // step_rows
    for q in range(chunks):
        value = project(q)
        place = pl.ds(q * step_rows, step_rows)
        bsend[place] = value[:, LANES : LANES + part].astype(BF16).reshape(step_rows, cols, part)
        scale_copy(q).start()
        bown[place] = value[:, 0:part].reshape(step_rows, cols, part)

    gather(n_cols, c, hrecv, sem_h_s, sem_h_r, ch, "cols")
    gather(n_rows, r, vrecv, sem_v_s, sem_v_r, packed, "rows")
    for d in range(2):
        last = packed[d, cols : cols + cols // 2]
        cv[d, 0] = packed[d, 0:cols]
        cv[d, 1, 0 : cols // 2] = jnp.where(side, last, 0.0)
        cv[d, 1, cols // 2 : cols] = jnp.where(side, pltpu.roll(last, LANES // 2, 1), 0.0)

    lane = lax.broadcasted_iota(jnp.int32, (cols, LANES), 1)
    halves = st.shape[0]
    per_half = rows // halves

    def stat_copy(g):
        return pltpu.make_async_remote_copy(
            st.at[g], st_other.at[g], sem_st.at[0, g], sem_st.at[1, g], device_id=at(0, 0, o), device_id_type=MESH
        )

    def part_copy(q):
        place = pl.ds(q * step_rows, step_rows)
        return pltpu.make_async_remote_copy(
            psend.at[place], precv.at[place], sem_p.at[0, q], sem_p.at[1, q],
            device_id=at(0, 0, o), device_id_type=MESH,
        )

    inner = 2 * width
    for q in range(chunks):
        g = q * halves // chunks

        def total_row(i, stats):
            place = pl.ds(pl.multiple_of(i * cols, 8), cols)
            place_h = pl.ds(pl.multiple_of(i * pitch, 8), cols)
            one, two, values = 0.0, 0.0, []
            for t in range(tiles):
                across = (
                    ph[0, t, place_h, :] + ph[1, t, place_h, :]
                    + kh[0, t, place_h, :] * ch[0, t, pl.ds(i, 1), :]
                    + kh[1, t, place_h, :] * ch[1, t, pl.ds(i, 1), :]
                )
                along = (
                    pv[0, t, place, :] + pv[1, t, place, :]
                    + kv[0, t, place, :] * cv[0, t] + kv[1, t, place, :] * cv[1, t]
                )
                value = across + along.astype(BF16).astype(F32)
                values.append(value)
                one = one + value
                two = two + value * value
            one = jnp.sum(one, -1, keepdims=True)
            two = jnp.sum(two, -1, keepdims=True)
            mean = one / width
            for t in range(tiles):
                gated[place, t * LANES : (t + 1) * LANES] = ((values[t] - mean) * zs[t, place, :]).astype(BF16)
            at_lane = i - g * per_half
            return jnp.where(lane == at_lane, one, jnp.where(lane == per_half + at_lane, two, stats))

        stats = jnp.zeros((cols, LANES), F32) if q * halves % chunks == 0 else stats
        stats = lax.fori_loop(q * step_rows, (q + 1) * step_rows, total_row, stats, unroll=True)
        if (q + 1) * halves % chunks == 0:
            st[g] = stats
            stat_copy(g).start()
        value = project(q)
        place = pl.ds(q * step_rows, step_rows)
        psend[place] = value[:, LANES : LANES + part].astype(BF16).reshape(step_rows, cols, part)
        part_copy(q).start()
        pown[place] = value[:, 0:part].reshape(step_rows, cols, part)

    for q in range(chunks):
        scale_copy(q).wait_recv()
    for q in range(chunks):
        g = q * halves // chunks
        if q * halves % chunks == 0:
            stat_copy(g).wait_recv()
            mine, both = st[g], st[g] + st_other[g]
            mean = both / inner
            msq = pltpu.roll(both, LANES - per_half, 1) / inner
            rstd = lax.rsqrt(msq - mean * mean + 1e-05)
            shift = rstd * (mine / width - mean)
        part_copy(q).wait_recv()
        for i in range(q * step_rows, (q + 1) * step_rows):
            at_lane = i - g * per_half
            scale = jnp.broadcast_to(rstd[:, at_lane : at_lane + 1], (cols, part))
            offset = jnp.broadcast_to(shift[:, at_lane : at_lane + 1], (cols, part))
            own = (scale * pown[i] + offset * bown[i]).astype(BF16).astype(F32)
            other = (scale * precv[i].astype(F32) - offset * brecv[i].astype(F32)).astype(BF16).astype(F32)
            out[i] = (tok[i].astype(F32) + (2.0 * half_mask) * (own + other)).astype(BF16)

    for g in range(bands):
        tok_copy(g).wait_send()
    for n, (present, *_rest) in enumerate(neighbours):

        @pl.when(present)
        def _():
            for turn, chan in enumerate((k, o)):
                halo_copy(n, turn, chan).wait_send()

    all_totals(lambda copy: copy.wait_send(), *vertical_set)
    all_totals(lambda copy: copy.wait_send(), *horizontal_set)
    for g in range(halves):
        stat_copy(g).wait_send()
    for q in range(chunks):
        part_copy(q).wait_send()
        scale_copy(q).wait_send()


def on_device(
    n_rows, n_cols,
    tokens, tile_mask, ln_gain, w_in_x, w_in_z, conv_w, conv_b, gate_scale, gate_bias, norm_gain, w_out,
):
    rows, cols, part = tokens.shape
    width = w_in_x.shape[1]
    tiles = -(-width // LANES)
    pad = tiles * LANES
    tall = rows * cols
    pitch = cols + 8
    assert TILE % rows == 0 and TILE % cols == 0 and 2 * width == 3 * LANES
    halo_rows = 2 * cols + 2 * rows + 64
    dma = pltpu.SemaphoreType.DMA
    vmem = pl.BlockSpec(memory_space=pltpu.VMEM)
    chunks = rows // 4
    operands = (
        tokens, tile_mask, ln_gain.reshape(1, -1), w_in_x, w_in_z, conv_w, conv_b.reshape(1, -1),
        gate_scale, gate_bias, norm_gain.reshape(1, -1), w_out,
    )
    scratch = [
        (pltpu.SMEM if n == 1 else pltpu.VMEM)(x.shape, x.dtype) for n, x in enumerate(operands)
    ] + [
        dma((len(operands),)),
        pltpu.SemaphoreType.REGULAR((2, 2, max(n_rows, n_cols, 3))),

        pltpu.VMEM((rows, cols, part), BF16),
        pltpu.VMEM((rows * 32, LANES), F32),
        pltpu.VMEM((2 * rows, part), BF16),
        pltpu.VMEM((2, halo_rows, part), BF16),
        pltpu.VMEM((2, part, pad), BF16),
        pltpu.VMEM((2, part, pad), BF16),
        pltpu.VMEM((pad, 2 * LANES), BF16),
        pltpu.VMEM((16, pad), F32),
        pltpu.VMEM((tiles, 8, LANES), F32),
        pltpu.VMEM((2, rows, cols, part), BF16),
        pltpu.VMEM((halo_rows, pad), F32),
        pltpu.VMEM((tiles, rows + 2, cols + 16, LANES), F32),
        pltpu.VMEM((tiles, rows * pitch, LANES), F32),
        pltpu.VMEM((2, tiles, tall, LANES), F32),
        pltpu.VMEM((2, tiles, tall, LANES), F32),
        pltpu.VMEM((2, tiles, rows * pitch, LANES), F32),
        pltpu.VMEM((2, tiles, rows * pitch, LANES), F32),
        pltpu.VMEM((tiles, tall, LANES), F32),
        pltpu.VMEM((tall, pad), BF16),
        pltpu.VMEM((2, 2, tiles, cols, LANES), F32),
        pltpu.VMEM((2, cols * 3 // 2, LANES), F32),
        pltpu.VMEM((2, 2, cols * 3 // 2, LANES), BF16),
        pltpu.VMEM((n_rows, 2, cols * 3 // 2, LANES), BF16),
        pltpu.VMEM((2, 2, tiles, rows, LANES), BF16),
        pltpu.VMEM((n_cols, 2, tiles, rows, LANES), BF16),
        pltpu.VMEM((2, tiles, cols, LANES), F32),
        pltpu.VMEM((2, tiles, rows, LANES), F32),
        pltpu.VMEM((2, cols, LANES), F32),
        pltpu.VMEM((2, cols, LANES), F32),
        pltpu.VMEM((rows, cols, part), BF16),
        pltpu.VMEM((rows, cols, part), BF16),
        pltpu.VMEM((rows, cols, part), F32),
        pltpu.VMEM((rows, cols, part), BF16),
        pltpu.VMEM((rows, cols, part), BF16),
        pltpu.VMEM((rows, cols, part), F32),
        dma((2, 2)),
        dma((8, 2)),
        dma((8, 2)),
        dma((2, n_rows)),
        dma((n_rows,)),
        dma((2, n_cols)),
        dma((n_cols,)),
        dma((2, 2)),
        dma((2, chunks)),
        dma((2, chunks)),
    ]
    return pl.pallas_call(
        functools.partial(kernel, n_rows, n_cols, pitch),
        out_shape=pltpu.VMEM(tokens.shape, BF16),
        in_specs=[pl.BlockSpec(memory_space=pl.ANY)] * len(operands),
        out_specs=vmem,
        scratch_shapes=scratch,
        compiler_params=pltpu.CompilerParams(collective_id=0, has_side_effects=True),
    )(*operands)


def solution(mesh):
    in_specs = (
        P(("groups", "rows"), "cols", "chan"),
        P("groups", None),
        P(),
        P(None, "chan"),
        P(None, "chan"),
        P(None, None, "chan"),
        P("chan"),
        P(None, "chan"),
        P(None, "chan"),
        P("chan"),
        P("chan", None),
    )
    out_specs = P(("groups", "rows"), "cols", "chan")
    return jax.shard_map(
        functools.partial(on_device, mesh.shape["rows"], mesh.shape["cols"]),
        mesh=mesh, in_specs=in_specs, out_specs=out_specs, check_vma=False,
    )
```
